32 devices in a mesh: gx: 4 (over x, core), gy: 4 (over z), gz: 2 (over y).
Axes of the slice: x: 2, y: 2, z: 4, core: 2. Of those that a mesh axis runs over, the one named last changes fastest.
Arguments:
- right_side: float32 [64, 32, 256], P('gx', 'gy', 'gz'), may hold values from -6 to 6
- inv_density: float32 [64, 32, 256], P('gx', 'gy', 'gz'), may hold values from 0.25 to 4
Outputs:
- pressure: float32 [64, 32, 256], P('gx', 'gy', 'gz')
- residual: float32 [64, 32, 256], P('gx', 'gy', 'gz')
The draws below stay inside these ranges and needn't reach their ends.
All inputs are finite; a program needn't handle non-finite values.
Results may differ from the reference program's by a relative error of at most 0.0003.
Values sent between devices are 32-bit elements; how exact they have to be, the bound alone decides.
A program may use at most 64 MiB of HBM per device.

```python
import math
import jax
import jax.numpy as jnp

LEVELS = 3
DEGREE = 2
COARSE_DEGREE = 6
NX = 64
NY = 32
NZ = 256


def draw_right_side(key, part):
    second = jax.random.fold_in(key, 1)
    values = jax.random.normal(second, (NX, NY, NZ), jnp.float32)
    return jnp.clip(values, -6.0, 6.0).astype(jnp.float32)


def block_scale(stream_key, extent, cuts, smallest, top_value):
    gain = 1.0
    for dim, parts in cuts:
        draws = jax.random.uniform(jax.random.fold_in(jax.random.fold_in(stream_key, 6), dim), (parts,), jnp.float32, smallest / len(cuts), top_value / len(cuts))
        gain = gain * jnp.repeat(jnp.exp(draws), extent[dim] // parts).reshape((-1,) + (1,) * (len(extent) - 1 - dim))
    return gain


def setup_inputs(seed: int = 0) -> dict:
    splits = jax.random.split(jax.random.key(seed), 3)
    return {
        "right_side": draw_right_side(jax.random.fold_in(splits[2], 71), 0),
        "inv_density": jnp.clip(jnp.exp(math.log(4.0) - 2.7725887 * jax.random.uniform(splits[1], (NX, NY, NZ), jnp.float32) ** block_scale(splits[1], (NX, NY, NZ), ((0, 4), (1, 4), (2, 2)), -0.2, 0.2)), 0.25, 4.0),
    }


def mean_cells(field):
    n, m, k = field.shape
    return field.reshape(n // 2, 2, m // 2, 2, k // 2, 2).sum(axis=(1, 3, 5)) * 0.125


def copy_cells(field):
    return jnp.repeat(jnp.repeat(jnp.repeat(field, 2, 0), 2, 1), 2, 2)


def harmonic(first, second):
    inside = first * second > 0.0
    return jnp.where(inside, 2.0 * first * second / (first + second), first + second)


def face_coefs(padded):
    face_x = harmonic(padded[:-1, 1:-1, 1:-1], padded[1:, 1:-1, 1:-1])
    face_y = harmonic(padded[1:-1, :-1, 1:-1], padded[1:-1, 1:, 1:-1])
    face_z = harmonic(padded[1:-1, 1:-1, :-1], padded[1:-1, 1:-1, 1:])
    return face_x, face_y, face_z


def operate(padded, faces, scale):
    face_x, face_y, face_z = faces
    center = padded[1:-1, 1:-1, 1:-1]
    total = face_x[1:] * (center - padded[2:, 1:-1, 1:-1])
    total = total + face_x[:-1] * (center - padded[:-2, 1:-1, 1:-1])
    total = total + face_y[:, 1:] * (center - padded[1:-1, 2:, 1:-1])
    total = total + face_y[:, :-1] * (center - padded[1:-1, :-2, 1:-1])
    total = total + face_z[:, :, 1:] * (center - padded[1:-1, 1:-1, 2:])
    total = total + face_z[:, :, :-1] * (center - padded[1:-1, 1:-1, :-2])
    return scale * total


def inverse_diag(faces, scale):
    face_x, face_y, face_z = faces
    total = face_x[1:] + face_x[:-1] + face_y[:, 1:] + face_y[:, :-1] + face_z[:, :, 1:] + face_z[:, :, :-1]
    return 1.0 / (scale * total)


def chebyshev(start, source, steps, lower, upper, apply_op, inv_diag):
    theta = (upper + lower) / 2.0
    delta = (upper - lower) / 2.0
    sigma = theta / delta
    rho_now = 1.0 / sigma
    if start is None:
        remain = source
        solution = jnp.zeros_like(source)
    else:
        remain = source - apply_op(start)
        solution = start
    update = remain * inv_diag / theta
    solution = solution + update
    for index in range(steps - 1):
        rho_next = 1.0 / (2.0 * sigma - rho_now)
        remain = source - apply_op(solution)
        update = rho_next * rho_now * update + (2.0 * rho_next / delta) * (remain * inv_diag)
        solution = solution + update
        rho_now = rho_next
    return solution


def vcycle(depth, source, coef):
    scale = 0.25 ** depth
    faces = face_coefs(jnp.pad(coef, 1))
    inv_diag = inverse_diag(faces, scale)

    def apply_op(field):
        return operate(jnp.pad(field, 1), faces, scale)

    if depth == LEVELS:
        return chebyshev(None, source, COARSE_DEGREE, 0.05, 2.0, apply_op, inv_diag), apply_op
    solution = chebyshev(None, source, DEGREE, 0.3, 2.0, apply_op, inv_diag)
    remain = source - apply_op(solution)
    correction, unused = vcycle(depth + 1, mean_cells(remain), mean_cells(coef))
    solution = solution + copy_cells(correction)
    solution = chebyshev(solution, source, DEGREE, 0.3, 2.0, apply_op, inv_diag)
    return solution, apply_op


def reference(right_side, inv_density):
    pressure, apply_op = vcycle(0, right_side, inv_density)
    return pressure, right_side - apply_op(pressure)
```

```python
import functools

import jax
import jax.numpy as jnp
from jax import lax
from jax.experimental import pallas as pl
from jax.experimental.pallas import tpu as pltpu
from jax.sharding import PartitionSpec as P

COARSE_DEGREE = 6
AXES = ("gx", "gy", "gz")
LANES = 128
TILE = 8
MESH = pl.DeviceIdType.MESH
F32 = jnp.float32


def div(a, n):
    if n & (n - 1) == 0:
        return lax.shift_right_logical(a, jnp.int32(n.bit_length() - 1))
    return a // n


def mod(a, n):
    if n & (n - 1) == 0:
        return a & jnp.int32(n - 1)
    return a % n


def iota(shape, dim):
    return lax.broadcasted_iota(jnp.int32, shape, dim)


def dot(a, b):
    return lax.dot(a, b, precision=lax.Precision.HIGHEST, preferred_element_type=F32)


def up8(n):
    return -(-n // TILE) * TILE


def upl(n):
    return -(-n // LANES) * LANES


def restrict(v, dims, width_out, offset):
    x, y, z = dims
    rows, cols = (x // 2) * (y // 2), x * y
    r, s = iota((rows, cols), 0), iota((rows, cols), 1)
    hit = (div(div(s, y), 2) == div(r, y // 2)) & (div(mod(s, y), 2) == mod(r, y // 2))
    left = jnp.where(hit, 0.125, 0.0).astype(F32)
    k, l = iota((v.shape[1], width_out), 0), iota((v.shape[1], width_out), 1)
    right = jnp.where((l == div(k, 2) + offset) & (k < z), 1.0, 0.0).astype(F32)
    return dot(dot(left, v), right)


def prolong(e, dims, width_out, coarse_y, x0, y0, z0):
    x, y, z = dims
    rows, cols = x * y, e.shape[0]
    r, s = iota((rows, cols), 0), iota((rows, cols), 1)
    want = (div(div(r, y), 2) + x0) * coarse_y + div(mod(r, y), 2) + y0
    left = jnp.where(s == want, 1.0, 0.0).astype(F32)
    k, l = iota((e.shape[1], width_out), 0), iota((e.shape[1], width_out), 1)
    right = jnp.where((k == div(l, 2) + z0) & (l < z), 1.0, 0.0).astype(F32)
    return dot(dot(left, e), right)


def harmonic(a, b):
    return 2.0 * a * b / (a + b)


def make_coefs(c, around, edges, scale):
    links, total = [], None
    for near, edge in zip(around, edges):
        face = harmonic(c, jnp.where(edge, c, near))
        total = face if total is None else total + face
        links.append(jnp.where(edge, 0.0, face) * scale)
    total = total * scale
    return links, total, 1.0 / total


def apply_op(v, around, coefs):
    links, total, unused = coefs
    out = total * v
    for near, link in zip(around, links):
        out = out - link * near
    return out


def chebyshev(start, source, steps, lower, upper, coefs, near_of):
    theta = (upper + lower) / 2.0
    delta = (upper - lower) / 2.0
    sigma = theta / delta
    rho_now = 1.0 / sigma
    inv = coefs[2]
    if start is None:
        update = source * inv * (1.0 / theta)
        field = update
    else:
        remain = source - apply_op(start, near_of(start), coefs)
        update = remain * inv * (1.0 / theta)
        field = start + update
    for index in range(steps - 1):
        rho_next = 1.0 / (2.0 * sigma - rho_now)
        remain = source - apply_op(field, near_of(field), coefs)
        update = rho_next * rho_now * update + (2.0 * rho_next / delta) * (remain * inv)
        field = field + update
        rho_now = rho_next
    return field


def kernel(sizes, dims0, b_ref, c_ref, p_ref, q_ref, *scratch):
    (v0, ys0, zs0, xr0, yr0, zr0, ey0, v1, ys1, zs1, xr1, yr1, zr1, ey1, tile, slots,
     send0, recv0, send1, recv1, gsend, grecv) = scratch
    pos = tuple(lax.axis_index(a) for a in AXES)
    dims1 = tuple(d // 2 for d in dims0)
    dims2 = tuple(d // 2 for d in dims1)
    whole2 = tuple(d * n for d, n in zip(dims2, sizes))
    whole3 = tuple(d // 2 for d in whole2)
    nx, ny, nz = sizes
    count = nx * ny * nz
    me = (pos[0] * ny + pos[1]) * nz + pos[2]
    width2, width3 = upl(whole2[2]), upl(whole3[2])

    def coords(index):
        return (index // (ny * nz), (index // nz) % ny, index % nz)

    barrier = pltpu.get_barrier_semaphore()

    def greet(step, unused):
        pl.semaphore_signal(barrier, inc=1, device_id=coords((me + step) % count), device_id_type=MESH)
        return unused

    for ref in (xr0, yr0, zr0, xr1, yr1, zr1, ey0, ey1):
        ref[...] = jnp.zeros_like(ref)
    lax.fori_loop(1, count, greet, 0)

    def exists(axis, side):
        return pos[axis] > 0 if side == 0 else pos[axis] < sizes[axis] - 1

    def peer(axis, side):
        return tuple(p + ((-1, 1)[side] if a == axis else 0) for a, p in enumerate(pos))

    def copies(level, slot):
        x, y, z = (dims0, dims1)[level]
        rows = x * y
        v, ys, zs, xr, yr, zr, send, recv = (
            (v0, ys0, zs0, xr0, yr0, zr0, send0, recv0),
            (v1, ys1, zs1, xr1, yr1, zr1, send1, recv1),
        )[level]
        edge = up8(y)
        for axis in range(3):
            for side in range(2):
                if axis == 0:
                    start = 0 if side == 0 else rows - edge
                    src, dst = v.at[slot, pl.ds(start, edge)], xr.at[slot, 1 - side]
                elif axis == 1:
                    src, dst = ys.at[slot, side], yr.at[slot, 1 - side]
                else:
                    src, dst = zs.at[slot, side], zr.at[slot, 1 - side]
                yield axis, side, pltpu.make_async_remote_copy(
                    src_ref=src, dst_ref=dst,
                    send_sem=send.at[slot, 2 * axis + side],
                    recv_sem=recv.at[slot, 2 * axis + 1 - side],
                    device_id=peer(axis, side), device_id_type=MESH,
                )

    def post(level, slot, value):
        x, y, z = (dims0, dims1)[level]
        rows = x * y
        v, ys, zs = ((v0, ys0, zs0), (v1, ys1, zs1))[level]
        v[slot] = value
        for side in range(2):
            ys[slot, side] = v[slot, pl.ds(0 if side == 0 else y - 1, x, stride=y), :]
            lane = iota((TILE, LANES), 1)
            packed = jnp.zeros((TILE, LANES), F32)
            for t in range(rows // TILE):
                part = value[t * TILE:(t + 1) * TILE]
                shift = (t if side == 0 else t - (z - 1)) % LANES
                if shift:
                    part = pltpu.roll(part, shift, 1)
                packed = jnp.where(lane == t, part, packed)
            zs[slot, side] = packed
        for axis, side, copy in copies(level, slot):
            @pl.when(exists(axis, side))
            def _():
                copy.start()

    def drain(level, slot):
        for axis, side, copy in copies(level, slot):
            @pl.when(exists(axis, side))
            def _():
                copy.wait_send()

    def collect(level, slot, value):
        x, y, z = (dims0, dims1)[level]
        rows = x * y
        xr, yr, zr, ey, recv = ((xr0, yr0, zr0, ey0, recv0), (xr1, yr1, zr1, ey1, recv1))[level]
        for axis in range(3):
            for side in range(2):
                dst = (xr, yr, zr)[axis].at[slot, side]
                @pl.when(exists(axis, side))
                def _():
                    pltpu.make_async_copy(dst, dst, recv.at[slot, 2 * axis + side]).wait()
        edge = up8(y)
        below = jnp.concatenate([xr[slot, 0], value], 0)[edge - y:edge - y + rows]
        above = jnp.concatenate([value, xr[slot, 1]], 0)[y:y + rows]
        ey[slot, 0, pl.ds(0, x, stride=y), :] = yr[slot, 0]
        ey[slot, 1, pl.ds(y - 1, x, stride=y), :] = yr[slot, 1]
        row = mod(iota((rows, LANES), 0), y)
        lane = iota((rows, LANES), 1)
        left = jnp.where(row == 0, ey[slot, 0], pltpu.roll(value, 1, 0))
        right = jnp.where(row == y - 1, ey[slot, 1], pltpu.roll(value, rows - 1, 0))

        def unpack(part, place):
            out = []
            for t in range(rows // TILE):
                shift = (place - t) % LANES
                out.append(pltpu.roll(part, shift, 1) if shift else part)
            return jnp.concatenate(out, 0)

        front = jnp.where(lane == 0, unpack(zr[slot, 0], 0), pltpu.roll(value, 1, 1))
        back = jnp.where(lane == z - 1, unpack(zr[slot, 1], z - 1), pltpu.roll(value, LANES - 1, 1))
        return (below, above, left, right, front, back)

    def local_edges(dims):
        x, y, z = dims
        rows = x * y
        plane, row, lane = div(iota((rows, LANES), 0), y), mod(iota((rows, LANES), 0), y), iota((rows, LANES), 1)
        return tuple(
            index + pos[axis] * dims[axis] == (0 if side == 0 else dims[axis] * sizes[axis] - 1)
            for axis, index in enumerate((plane, row, lane)) for side in range(2)
        )

    def whole_edges(dims, shape):
        x, y, z = dims
        plane, row, lane = div(iota(shape, 0), y), mod(iota(shape, 0), y), iota(shape, 1)
        return (plane == 0, plane == x - 1, row == 0, row == y - 1, lane == 0, lane >= z - 1)

    def whole_near(dims):
        x, y, z = dims
        rows = x * y

        def near(v):
            return (
                pltpu.roll(v, y, 0), pltpu.roll(v, rows - y, 0),
                pltpu.roll(v, 1, 0), pltpu.roll(v, rows - 1, 0),
                pltpu.roll(v, 1, 1), pltpu.roll(v, v.shape[1] - 1, 1),
            )
        return near

    def gather_copy(kind, step):
        target = coords((me + step) % count)
        return pltpu.make_async_remote_copy(
            src_ref=tile.at[kind], dst_ref=slots.at[kind, me],
            send_sem=gsend.at[kind], recv_sem=grecv.at[kind],
            device_id=target, device_id_type=MESH,
        )

    def gather_start(kind, value):
        tile[kind] = value

        def go(step, unused):
            gather_copy(kind, step).start()
            return unused
        lax.fori_loop(1, count, go, 0)

    def gather_finish(kind):
        part = slots.at[kind, pl.ds(0, count - 1)]
        pltpu.make_async_copy(part, part, grecv.at[kind]).wait()
        slots[kind, me] = tile[kind]
        per = LANES // dims2[2]
        block = dims2[0] * dims2[1]
        columns = []
        for lane_tile in range(width2 // LANES):
            rows = []
            for gx in range(nx):
                for gy in range(ny):
                    total = None
                    for gz in range(lane_tile * per, min((lane_tile + 1) * per, nz)):
                        part = slots[kind, (gx * ny + gy) * nz + gz]
                        total = part if total is None else total + part
                    rows.append(total)
            columns.append(jnp.concatenate(rows, 0))
        stacked = columns[0] if len(columns) == 1 else jnp.concatenate(columns, 1)
        n = whole2[0] * whole2[1]
        r, s = iota((n, n), 0), iota((n, n), 1)
        X, Y = div(r, whole2[1]), mod(r, whole2[1])
        want = (div(X, dims2[0]) * ny + div(Y, dims2[1])) * block + mod(X, dims2[0]) * dims2[1] + mod(Y, dims2[1])
        return dot(jnp.where(s == want, 1.0, 0.0).astype(F32), stacked)

    offset = (pos[2] % (LANES // dims2[2])) * dims2[2]

    def fill(c, dims):
        return jnp.where(iota(c.shape, 1) < dims[2], c, 1.0)

    c0 = c_ref[...].reshape(dims0[0] * dims0[1], LANES)
    b0 = b_ref[...].reshape(dims0[0] * dims0[1], LANES)
    c1 = restrict(c0, dims0, LANES, 0)
    c2_own = restrict(c1, dims1, LANES, offset)
    c1 = fill(c1, dims1)
    pl.semaphore_wait(barrier, count - 1)

    post(0, 0, c0)
    post(1, 0, c1)
    gather_start(0, c2_own)

    coefs0 = make_coefs(c0, collect(0, 0, c0), local_edges(dims0), 1.0)

    def near_at(level, slots_used):
        queue = list(slots_used)

        def near(v):
            slot = queue.pop(0)
            post(level, slot, v)
            return collect(level, slot, v)
        return near

    near0 = near_at(0, range(1, 6))
    x0 = chebyshev(None, b0, 2, 0.3, 2.0, coefs0, near0)
    r0 = b0 - apply_op(x0, near0(x0), coefs0)
    b1 = restrict(r0, dims0, LANES, 0)

    coefs1 = make_coefs(c1, collect(1, 0, c1), local_edges(dims1), 0.25)
    near1 = near_at(1, range(1, 5))
    x1 = chebyshev(None, b1, 2, 0.3, 2.0, coefs1, near1)
    r1 = b1 - apply_op(x1, near1(x1), coefs1)
    gather_start(1, restrict(r1, dims1, LANES, offset))

    c2 = gather_finish(0)
    shape2 = (whole2[0] * whole2[1], width2)
    near2 = whole_near(whole2)
    c3 = fill(restrict(c2, whole2, width3, 0), whole3)
    c2 = fill(c2, whole2)
    coefs2 = make_coefs(c2, near2(c2), whole_edges(whole2, shape2), 0.25 ** 2)
    near3 = whole_near(whole3)
    coefs3 = make_coefs(c3, near3(c3), whole_edges(whole3, c3.shape), 0.25 ** 3)

    b2 = gather_finish(1)
    x2 = chebyshev(None, b2, 2, 0.3, 2.0, coefs2, near2)
    r2 = b2 - apply_op(x2, near2(x2), coefs2)
    b3 = restrict(r2, whole2, width3, 0)
    x3 = chebyshev(None, b3, COARSE_DEGREE, 0.05, 2.0, coefs3, near3)
    x2 = x2 + prolong(x3, whole2, width2, whole3[1], 0, 0, 0)
    x2 = chebyshev(x2, b2, 2, 0.3, 2.0, coefs2, near2)

    x1 = x1 + prolong(x2, dims1, LANES, whole2[1], pos[0] * dims2[0], pos[1] * dims2[1], pos[2] * dims2[2])
    x1 = chebyshev(x1, b1, 2, 0.3, 2.0, coefs1, near1)
    x0 = x0 + prolong(x1, dims0, LANES, dims1[1], 0, 0, 0)
    x0 = chebyshev(x0, b0, 2, 0.3, 2.0, coefs0, near0)
    p_ref[...] = x0.reshape(p_ref.shape)
    res = b0 - apply_op(x0, near0(x0), coefs0)
    q_ref[...] = res.reshape(q_ref.shape)

    for slot in range(6):
        drain(0, slot)
    for slot in range(5):
        drain(1, slot)
    for kind in range(2):
        part = slots.at[kind, pl.ds(0, count - 1)]
        pltpu.make_async_copy(part, part, gsend.at[kind]).wait()


def solution(mesh):
    sizes = tuple(mesh.shape[a] for a in AXES)
    count = sizes[0] * sizes[1] * sizes[2]

    def per_device(b, c):
        dims0 = b.shape
        scratch = []
        for slots, (x, y, z) in ((6, dims0), (5, tuple(d // 2 for d in dims0))):
            scratch += [
                pltpu.VMEM((slots, x * y, LANES), F32),
                pltpu.VMEM((slots, 2, x, LANES), F32),
                pltpu.VMEM((slots, 2, TILE, LANES), F32),
                pltpu.VMEM((slots, 2, up8(y), LANES), F32),
                pltpu.VMEM((slots, 2, x, LANES), F32),
                pltpu.VMEM((slots, 2, TILE, LANES), F32),
                pltpu.VMEM((slots, 2, x * y, LANES), F32),
            ]
        scratch += [
            pltpu.VMEM((2, TILE, LANES), F32),
            pltpu.VMEM((2, count, TILE, LANES), F32),
            pltpu.SemaphoreType.DMA((6, 6)), pltpu.SemaphoreType.DMA((6, 6)),
            pltpu.SemaphoreType.DMA((5, 6)), pltpu.SemaphoreType.DMA((5, 6)),
            pltpu.SemaphoreType.DMA((2,)), pltpu.SemaphoreType.DMA((2,)),
        ]
        shape = jax.ShapeDtypeStruct(dims0, F32)
        return pl.pallas_call(
            functools.partial(kernel, sizes, dims0),
            out_shape=(shape, shape),
            in_specs=[pl.BlockSpec(memory_space=pltpu.VMEM)] * 2,
            out_specs=(pl.BlockSpec(memory_space=pltpu.VMEM),) * 2,
            scratch_shapes=scratch,
            compiler_params=pltpu.CompilerParams(collective_id=0, has_side_effects=True),
        )(b, c)

    spec = P(*AXES)
    return jax.shard_map(per_device, mesh=mesh, in_specs=(spec, spec), out_specs=(spec, spec), check_vma=False)
```

```python
import functools

import jax
import jax.numpy as jnp
from jax import lax
from jax.experimental import pallas as pl
from jax.experimental.pallas import tpu as pltpu
from jax.sharding import PartitionSpec as P

COARSE_DEGREE = 6
AXES = ("gx", "gy", "gz")
LANES = 128
TILE = 8
MESH = pl.DeviceIdType.MESH
F32 = jnp.float32


def div(a, n):
    if n & (n - 1) == 0:
        return lax.shift_right_logical(a, jnp.int32(n.bit_length() - 1))
    return a // n


def mod(a, n):
    if n & (n - 1) == 0:
        return a & jnp.int32(n - 1)
    return a % n


def iota(shape, dim):
    return lax.broadcasted_iota(jnp.int32, shape, dim)


def dot(a, b):
    return lax.dot(a, b, precision=lax.Precision.HIGHEST, preferred_element_type=F32)


def up8(n):
    return -(-n // TILE) * TILE


def upl(n):
    return -(-n // LANES) * LANES


def restrict(v, dims, width_out, offset):
    x, y, z = dims
    rows, cols = (x // 2) * (y // 2), x * y
    r, s = iota((rows, cols), 0), iota((rows, cols), 1)
    hit = (div(div(s, y), 2) == div(r, y // 2)) & (div(mod(s, y), 2) == mod(r, y // 2))
    left = jnp.where(hit, 0.125, 0.0).astype(F32)
    k, l = iota((v.shape[1], width_out), 0), iota((v.shape[1], width_out), 1)
    right = jnp.where((l == div(k, 2) + offset) & (k < z), 1.0, 0.0).astype(F32)
    return dot(dot(left, v), right)


def prolong(e, dims, width_out, coarse_y, x0, y0, z0):
    x, y, z = dims
    rows, cols = x * y, e.shape[0]
    r, s = iota((rows, cols), 0), iota((rows, cols), 1)
    want = (div(div(r, y), 2) + x0) * coarse_y + div(mod(r, y), 2) + y0
    left = jnp.where(s == want, 1.0, 0.0).astype(F32)
    k, l = iota((e.shape[1], width_out), 0), iota((e.shape[1], width_out), 1)
    right = jnp.where((k == div(l, 2) + z0) & (l < z), 1.0, 0.0).astype(F32)
    return dot(dot(left, e), right)


def prolong_near(dims, rows_in, width_in, coarse_y, x0, y0, z0):
    x, y, z = dims
    shape = (x * y, rows_in)
    i, j, s = div(iota(shape, 0), y), mod(iota(shape, 0), y), iota(shape, 1)
    lefts = []
    for sx, sy in ((0, 0), (-1, 0), (1, 0), (0, -1), (0, 1)):
        want = (div(i + (sx + 2), 2) + (x0 - 1)) * coarse_y + div(j + (sy + 2), 2) + (y0 - 1)
        lefts.append(jnp.where(s == want, 1.0, 0.0).astype(F32))
    k, l = iota((width_in, LANES), 0), iota((width_in, LANES), 1)
    rights = [
        jnp.where((k == div(l + (sz + 2), 2) + (z0 - 1)) & (l < z), 1.0, 0.0).astype(F32) for sz in (0, -1, 1)
    ]
    return jnp.concatenate(lefts, 0), rights


def harmonic(a, b):
    return 2.0 * a * b / (a + b)


def make_coefs(c, around, edges, scale):
    links, total = [], None
    for near, edge in zip(around, edges):
        face = harmonic(c, jnp.where(edge, c, near))
        total = face if total is None else total + face
        links.append(jnp.where(edge, 0.0, face) * scale)
    total = total * scale
    return links, total, 1.0 / total


def apply_op(v, around, coefs):
    links, total, unused = coefs
    out = total * v
    for near, link in zip(around, links):
        out = out - link * near
    return out


def chebyshev(start, source, steps, lower, upper, inv, op_of):
    theta = (upper + lower) / 2.0
    delta = (upper - lower) / 2.0
    sigma = theta / delta
    rho_now = 1.0 / sigma
    if start is None:
        update = source * inv * (1.0 / theta)
        field = update
    else:
        remain = source - op_of(start)
        update = remain * inv * (1.0 / theta)
        field = start + update
    for index in range(steps - 1):
        rho_next = 1.0 / (2.0 * sigma - rho_now)
        remain = source - op_of(field)
        update = rho_next * rho_now * update + (2.0 * rho_next / delta) * (remain * inv)
        field = field + update
        rho_now = rho_next
    return field


def kernel(sizes, dims0, b_ref, c_ref, p_ref, q_ref, *scratch):
    (v0, ys0, zs0, xr0, yr0, zr0, ey0, v1, ys1, zs1, xr1, yr1, zr1, ey1, tile, slots,
     send0, recv0, send1, recv1, gsend, grecv) = scratch
    pos = tuple(lax.axis_index(a) for a in AXES)
    dims1 = tuple(d // 2 for d in dims0)
    dims2 = tuple(d // 2 for d in dims1)
    whole2 = tuple(d * n for d, n in zip(dims2, sizes))
    whole3 = tuple(d // 2 for d in whole2)
    nx, ny, nz = sizes
    count = nx * ny * nz
    me = (pos[0] * ny + pos[1]) * nz + pos[2]
    width2, width3 = upl(whole2[2]), upl(whole3[2])

    def coords(index):
        return (index // (ny * nz), (index // nz) % ny, index % nz)

    barrier = pltpu.get_barrier_semaphore()

    def greet(step, unused):
        pl.semaphore_signal(barrier, inc=1, device_id=coords((me + step) % count), device_id_type=MESH)
        return unused

    for ref in (xr0, yr0, zr0, xr1, yr1, zr1, ey0, ey1):
        ref[...] = jnp.zeros_like(ref)
    lax.fori_loop(1, count, greet, 0)

    def exists(axis, side):
        return pos[axis] > 0 if side == 0 else pos[axis] < sizes[axis] - 1

    def peer(axis, side):
        return tuple(p + ((-1, 1)[side] if a == axis else 0) for a, p in enumerate(pos))

    def copies(level, slot):
        x, y, z = (dims0, dims1)[level]
        rows = x * y
        v, ys, zs, xr, yr, zr, send, recv = (
            (v0, ys0, zs0, xr0, yr0, zr0, send0, recv0),
            (v1, ys1, zs1, xr1, yr1, zr1, send1, recv1),
        )[level]
        edge = up8(y)
        for axis in range(3):
            for side in range(2):
                if axis == 0:
                    start = 0 if side == 0 else rows - edge
                    src, dst = v.at[slot, pl.ds(start, edge)], xr.at[slot, 1 - side]
                elif axis == 1:
                    src, dst = ys.at[slot, side], yr.at[slot, 1 - side]
                else:
                    src, dst = zs.at[slot, side], zr.at[slot, 1 - side]
                yield axis, side, pltpu.make_async_remote_copy(
                    src_ref=src, dst_ref=dst,
                    send_sem=send.at[slot, 2 * axis + side],
                    recv_sem=recv.at[slot, 2 * axis + 1 - side],
                    device_id=peer(axis, side), device_id_type=MESH,
                )

    def post(level, slot, value):
        x, y, z = (dims0, dims1)[level]
        rows = x * y
        v, ys, zs = ((v0, ys0, zs0), (v1, ys1, zs1))[level]
        v[slot] = value
        for side in range(2):
            ys[slot, side] = v[slot, pl.ds(0 if side == 0 else y - 1, x, stride=y), :]
            lane = iota((TILE, LANES), 1)
            packed = jnp.zeros((TILE, LANES), F32)
            for t in range(rows // TILE):
                part = value[t * TILE:(t + 1) * TILE]
                shift = (t if side == 0 else t - (z - 1)) % LANES
                if shift:
                    part = pltpu.roll(part, shift, 1)
                packed = jnp.where(lane == t, part, packed)
            zs[slot, side] = packed
        for axis, side, copy in copies(level, slot):
            @pl.when(exists(axis, side))
            def _():
                copy.start()

    def drain(level, slot):
        for axis, side, copy in copies(level, slot):
            @pl.when(exists(axis, side))
            def _():
                copy.wait_send()

    def arrive(level, slot):
        xr, yr, zr, recv = ((xr0, yr0, zr0, recv0), (xr1, yr1, zr1, recv1))[level]
        for axis in range(3):
            for side in range(2):
                dst = (xr, yr, zr)[axis].at[slot, side]
                @pl.when(exists(axis, side))
                def _():
                    pltpu.make_async_copy(dst, dst, recv.at[slot, 2 * axis + side]).wait()

    def unpack(part, place, rows):
        out = []
        for t in range(rows // TILE):
            shift = (place - t) % LANES
            out.append(pltpu.roll(part, shift, 1) if shift else part)
        return jnp.concatenate(out, 0)

    def collect(level, slot, value):
        arrive(level, slot)
        x, y, z = (dims0, dims1)[level]
        rows = x * y
        xr, yr, zr, ey = ((xr0, yr0, zr0, ey0), (xr1, yr1, zr1, ey1))[level]
        edge = up8(y)
        below = jnp.concatenate([xr[slot, 0], value], 0)[edge - y:edge - y + rows]
        above = jnp.concatenate([value, xr[slot, 1]], 0)[y:y + rows]
        ey[slot, 0, pl.ds(0, x, stride=y), :] = yr[slot, 0]
        ey[slot, 1, pl.ds(y - 1, x, stride=y), :] = yr[slot, 1]
        row = mod(iota((rows, LANES), 0), y)
        lane = iota((rows, LANES), 1)
        left = jnp.where(row == 0, ey[slot, 0], pltpu.roll(value, 1, 0))
        right = jnp.where(row == y - 1, ey[slot, 1], pltpu.roll(value, rows - 1, 0))

        front = jnp.where(lane == 0, unpack(zr[slot, 0], 0, rows), pltpu.roll(value, 1, 1))
        back = jnp.where(lane == z - 1, unpack(zr[slot, 1], z - 1, rows), pltpu.roll(value, LANES - 1, 1))
        return (below, above, left, right, front, back)

    def local_edges(dims):
        x, y, z = dims
        rows = x * y
        plane, row, lane = div(iota((rows, LANES), 0), y), mod(iota((rows, LANES), 0), y), iota((rows, LANES), 1)
        return tuple(
            index + pos[axis] * dims[axis] == (0 if side == 0 else dims[axis] * sizes[axis] - 1)
            for axis, index in enumerate((plane, row, lane)) for side in range(2)
        )

    def whole_edges(dims, shape):
        x, y, z = dims
        plane, row, lane = div(iota(shape, 0), y), mod(iota(shape, 0), y), iota(shape, 1)
        return (plane == 0, plane == x - 1, row == 0, row == y - 1, lane == 0, lane >= z - 1)

    def whole_near(dims):
        x, y, z = dims
        rows = x * y

        def near(v):
            return (
                pltpu.roll(v, y, 0), pltpu.roll(v, rows - y, 0),
                pltpu.roll(v, 1, 0), pltpu.roll(v, rows - 1, 0),
                pltpu.roll(v, 1, 1), pltpu.roll(v, v.shape[1] - 1, 1),
            )
        return near

    def gather_copy(kind, step):
        target = coords((me + step) % count)
        return pltpu.make_async_remote_copy(
            src_ref=tile.at[kind], dst_ref=slots.at[kind, me],
            send_sem=gsend.at[kind], recv_sem=grecv.at[kind],
            device_id=target, device_id_type=MESH,
        )

    def gather_start(kind, value):
        tile[kind] = value

        def go(step, unused):
            gather_copy(kind, step).start()
            return unused
        lax.fori_loop(1, count, go, 0)

    def gather_finish(kind):
        part = slots.at[kind, pl.ds(0, count - 1)]
        pltpu.make_async_copy(part, part, grecv.at[kind]).wait()
        slots[kind, me] = tile[kind]
        per = LANES // dims2[2]
        block = dims2[0] * dims2[1]
        columns = []
        for lane_tile in range(width2 // LANES):
            rows = []
            for gx in range(nx):
                for gy in range(ny):
                    total = None
                    for gz in range(lane_tile * per, min((lane_tile + 1) * per, nz)):
                        part = slots[kind, (gx * ny + gy) * nz + gz]
                        total = part if total is None else total + part
                    rows.append(total)
            columns.append(jnp.concatenate(rows, 0))
        stacked = columns[0] if len(columns) == 1 else jnp.concatenate(columns, 1)
        n = whole2[0] * whole2[1]
        r, s = iota((n, n), 0), iota((n, n), 1)
        X, Y = div(r, whole2[1]), mod(r, whole2[1])
        want = (div(X, dims2[0]) * ny + div(Y, dims2[1])) * block + mod(X, dims2[0]) * dims2[1] + mod(Y, dims2[1])
        return dot(jnp.where(s == want, 1.0, 0.0).astype(F32), stacked)

    offset = (pos[2] % (LANES // dims2[2])) * dims2[2]

    def fill(c, dims):
        return jnp.where(iota(c.shape, 1) < dims[2], c, 1.0)

    c0 = c_ref[...].reshape(dims0[0] * dims0[1], LANES)
    b0 = b_ref[...].reshape(dims0[0] * dims0[1], LANES)
    c1 = restrict(c0, dims0, LANES, 0)
    c2_own = restrict(c1, dims1, LANES, offset)
    c1 = fill(c1, dims1)
    pl.semaphore_wait(barrier, count - 1)

    post(0, 0, c0)
    post(1, 0, c1)
    gather_start(0, c2_own)

    lane0, row0, plane0 = (iota((dims0[0] * dims0[1], LANES), 1), mod(iota((dims0[0] * dims0[1], LANES), 0), dims0[1]),
                           div(iota((dims0[0] * dims0[1], LANES), 0), dims0[1]))
    sides0 = (plane0 == 0, plane0 == dims0[0] - 1, row0 == 0, row0 == dims0[1] - 1, lane0 == 0, lane0 == dims0[2] - 1)
    near0 = whole_near(dims0)
    near2, near3 = whole_near(whole2), whole_near(whole3)
    rows0, edge0 = dims0[0] * dims0[1], dims0[1]
    shape2 = (whole2[0] * whole2[1], width2)
    store = {}

    links0, total0, inv0 = make_coefs(c0, collect(0, 0, c0), local_edges(dims0), 1.0)
    inner0 = [jnp.where(side, 0.0, link) for side, link in zip(sides0, links0)]
    outer0 = [jnp.where(side, link, 0.0) for side, link in zip(sides0, links0)]

    def op0(slot, filler=None):
        def op(v):
            post(0, slot, v)
            out = apply_op(v, near0(v), (inner0, total0, None))
            if filler is not None:
                filler()
            arrive(0, slot)
            ey0[slot, 0, pl.ds(0, dims0[0], stride=edge0), :] = yr0[slot, 0]
            ey0[slot, 1, pl.ds(edge0 - 1, dims0[0], stride=edge0), :] = yr0[slot, 1]
            out = out - outer0[2] * ey0[slot, 0] - outer0[3] * ey0[slot, 1]
            out = out - outer0[4] * unpack(zr0[slot, 0], 0, rows0)
            out = out - outer0[5] * unpack(zr0[slot, 1], dims0[2] - 1, rows0)
            return jnp.concatenate([
                out[:edge0] - outer0[0][:edge0] * xr0[slot, 0],
                out[edge0:rows0 - edge0],
                out[rows0 - edge0:] - outer0[1][rows0 - edge0:] * xr0[slot, 1],
            ], 0)
        return op

    def ops(*steps):
        queue = list(steps)
        return lambda v: queue.pop(0)(v)

    def op1(slot, filler=None):
        def op(v):
            post(1, slot, v)
            if filler is not None:
                filler()
            store["near1"] = collect(1, slot, v)
            return apply_op(v, store["near1"], store["coefs1"])
        return op

    def fill_coefs1():
        store["coefs1"] = make_coefs(c1, collect(1, 0, c1), local_edges(dims1), 0.25)

    def fill_gather():
        store["c2"] = gather_finish(0)

    def fill_coefs2():
        c2 = store["c2"]
        store["c3"] = fill(restrict(c2, whole2, width3, 0), whole3)
        c2 = fill(c2, whole2)
        store["coefs2"] = make_coefs(c2, near2(c2), whole_edges(whole2, shape2), 0.25 ** 2)

    def fill_coefs3():
        c3 = store["c3"]
        store["coefs3"] = make_coefs(c3, near3(c3), whole_edges(whole3, c3.shape), 0.25 ** 3)
        store["prolong"] = prolong_near(
            dims1, shape2[0], width2, whole2[1], pos[0] * dims2[0], pos[1] * dims2[1], pos[2] * dims2[2])

    x0 = chebyshev(None, b0, 2, 0.3, 2.0, inv0, op0(1, fill_coefs1))
    r0 = b0 - op0(2, fill_gather)(x0)
    b1 = restrict(r0, dims0, LANES, 0)

    coefs1 = store["coefs1"]
    x1 = chebyshev(None, b1, 2, 0.3, 2.0, coefs1[2], op1(1, fill_coefs2))
    r1 = b1 - op1(2, fill_coefs3)(x1)
    gather_start(1, restrict(r1, dims1, LANES, offset))
    coefs2, coefs3, left5, rights = store["coefs2"], store["coefs3"], *store["prolong"]

    def op2(v):
        return apply_op(v, near2(v), coefs2)

    def op3(v):
        return apply_op(v, near3(v), coefs3)

    b2 = gather_finish(1)
    x2 = chebyshev(None, b2, 2, 0.3, 2.0, coefs2[2], op2)
    r2 = b2 - op2(x2)
    b3 = restrict(r2, whole2, width3, 0)
    x3 = chebyshev(None, b3, COARSE_DEGREE, 0.05, 2.0, coefs3[2], op3)
    x2 = x2 + prolong(x3, whole2, width2, whole3[1], 0, 0, 0)
    x2 = chebyshev(x2, b2, 2, 0.3, 2.0, coefs2[2], op2)

    rows1 = dims1[0] * dims1[1]
    picked = dot(left5, x2)
    spread = dot(picked, rights[0])
    near_e = [spread[n * rows1:(n + 1) * rows1] for n in range(1, 5)] + [dot(picked[:rows1], m) for m in rights[1:]]
    near_x = store["near1"]

    def op1_known(v):
        return apply_op(v, [a + b for a, b in zip(near_x, near_e)], coefs1)

    x1 = x1 + spread[:rows1]
    x1 = chebyshev(x1, b1, 2, 0.3, 2.0, coefs1[2], ops(op1_known, op1(3)))
    x0 = x0 + prolong(x1, dims0, LANES, dims1[1], 0, 0, 0)
    x0 = chebyshev(x0, b0, 2, 0.3, 2.0, inv0, ops(op0(3), op0(4)))
    p_ref[...] = x0.reshape(p_ref.shape)
    res = b0 - op0(5)(x0)
    q_ref[...] = res.reshape(q_ref.shape)

    for slot in range(6):
        drain(0, slot)
    for slot in range(4):
        drain(1, slot)
    for kind in range(2):
        part = slots.at[kind, pl.ds(0, count - 1)]
        pltpu.make_async_copy(part, part, gsend.at[kind]).wait()


def solution(mesh):
    sizes = tuple(mesh.shape[a] for a in AXES)
    count = sizes[0] * sizes[1] * sizes[2]

    def per_device(b, c):
        dims0 = b.shape
        scratch = []
        for slots, (x, y, z) in ((6, dims0), (4, tuple(d // 2 for d in dims0))):
            scratch += [
                pltpu.VMEM((slots, x * y, LANES), F32),
                pltpu.VMEM((slots, 2, x, LANES), F32),
                pltpu.VMEM((slots, 2, TILE, LANES), F32),
                pltpu.VMEM((slots, 2, up8(y), LANES), F32),
                pltpu.VMEM((slots, 2, x, LANES), F32),
                pltpu.VMEM((slots, 2, TILE, LANES), F32),
                pltpu.VMEM((slots, 2, x * y, LANES), F32),
            ]
        scratch += [
            pltpu.VMEM((2, TILE, LANES), F32),
            pltpu.VMEM((2, count, TILE, LANES), F32),
            pltpu.SemaphoreType.DMA((6, 6)), pltpu.SemaphoreType.DMA((6, 6)),
            pltpu.SemaphoreType.DMA((4, 6)), pltpu.SemaphoreType.DMA((4, 6)),
            pltpu.SemaphoreType.DMA((2,)), pltpu.SemaphoreType.DMA((2,)),
        ]
        shape = jax.ShapeDtypeStruct(dims0, F32)
        return pl.pallas_call(
            functools.partial(kernel, sizes, dims0),
            out_shape=(shape, shape),
            in_specs=[pl.BlockSpec(memory_space=pltpu.VMEM)] * 2,
            out_specs=(pl.BlockSpec(memory_space=pltpu.VMEM),) * 2,
            scratch_shapes=scratch,
            compiler_params=pltpu.CompilerParams(collective_id=0, has_side_effects=True),
        )(b, c)

    spec = P(*AXES)
    return jax.shard_map(per_device, mesh=mesh, in_specs=(spec, spec), out_specs=(spec, spec), check_vma=False)
```

```python
import functools

import jax
import jax.numpy as jnp
from jax import lax
from jax.experimental import pallas as pl
from jax.experimental.pallas import tpu as pltpu
from jax.sharding import PartitionSpec as P

COARSE_DEGREE = 6
AXES = ("gx", "gy", "gz")
LANES = 128
TILE = 8
MESH = pl.DeviceIdType.MESH
F32 = jnp.float32


def div(a, n):
    if n & (n - 1) == 0:
        return lax.shift_right_logical(a, jnp.int32(n.bit_length() - 1))
    return a // n


def mod(a, n):
    if n & (n - 1) == 0:
        return a & jnp.int32(n - 1)
    return a % n


def iota(shape, dim):
    return lax.broadcasted_iota(jnp.int32, shape, dim)


def parts(v):
    high = v.astype(jnp.bfloat16)
    rest = v - high.astype(F32)
    middle = rest.astype(jnp.bfloat16)
    return high, middle, (rest - middle.astype(F32)).astype(jnp.bfloat16)


def pick_rows(left, v):
    n = v.shape[1]
    out = lax.dot(left, jnp.concatenate(parts(v), 1), preferred_element_type=F32)
    return out[:, :n] + (out[:, n:2 * n] + out[:, 2 * n:])


def pick_lanes(v, right):
    n = v.shape[0]
    if n % 16:
        high, middle, low = (lax.dot(part, right, preferred_element_type=F32) for part in parts(v))
        return high + (middle + low)
    out = lax.dot(jnp.concatenate(parts(v), 0), right, preferred_element_type=F32)
    return out[:n] + (out[n:2 * n] + out[2 * n:])


def chosen(hit, value=1.0):
    return jnp.where(hit, value, 0.0).astype(jnp.bfloat16)


def up8(n):
    return -(-n // TILE) * TILE


def upl(n):
    return -(-n // LANES) * LANES


def restrict(v, dims, width_out, offset):
    x, y, z = dims
    rows, cols = (x // 2) * (y // 2), x * y
    r, s = iota((rows, cols), 0), iota((rows, cols), 1)
    hit = (div(div(s, y), 2) == div(r, y // 2)) & (div(mod(s, y), 2) == mod(r, y // 2))
    left = chosen(hit, 0.125)
    k, l = iota((v.shape[1], width_out), 0), iota((v.shape[1], width_out), 1)
    right = chosen((l == div(k, 2) + offset) & (k < z))
    return pick_lanes(pick_rows(left, v), right)


def prolong(e, dims, width_out, coarse_y, x0, y0, z0):
    x, y, z = dims
    rows, cols = x * y, e.shape[0]
    r, s = iota((rows, cols), 0), iota((rows, cols), 1)
    want = (div(div(r, y), 2) + x0) * coarse_y + div(mod(r, y), 2) + y0
    left = chosen(s == want)
    k, l = iota((e.shape[1], width_out), 0), iota((e.shape[1], width_out), 1)
    right = chosen((k == div(l, 2) + z0) & (l < z))
    return pick_lanes(pick_rows(left, e), right)


def prolong_near(dims, rows_in, width_in, coarse_y, x0, y0, z0):
    x, y, z = dims
    shape = (x * y, rows_in)
    i, j, s = div(iota(shape, 0), y), mod(iota(shape, 0), y), iota(shape, 1)
    lefts = []
    for sx, sy in ((0, 0), (-1, 0), (1, 0), (0, -1), (0, 1)):
        want = (div(i + (sx + 2), 2) + (x0 - 1)) * coarse_y + div(j + (sy + 2), 2) + (y0 - 1)
        lefts.append(chosen(s == want))
    k, l = iota((width_in, LANES), 0), iota((width_in, LANES), 1)
    rights = [
        chosen((k == div(l + (sz + 2), 2) + (z0 - 1)) & (l < z)) for sz in (0, -1, 1)
    ]
    return jnp.concatenate(lefts, 0), rights


def harmonic(a, b):
    return 2.0 * a * b / (a + b)


def make_coefs(c, around, edges, scale):
    links, total = [], None
    for near, edge in zip(around, edges):
        face = harmonic(c, jnp.where(edge, c, near))
        total = face if total is None else total + face
        links.append(jnp.where(edge, 0.0, face) * scale)
    total = total * scale
    return links, total, 1.0 / total


def apply_op(v, around, coefs):
    links, total, unused = coefs
    out = total * v
    for near, link in zip(around, links):
        out = out - link * near
    return out


def chebyshev(start, source, steps, lower, upper, inv, op_of):
    theta = (upper + lower) / 2.0
    delta = (upper - lower) / 2.0
    sigma = theta / delta
    rho_now = 1.0 / sigma
    if start is None:
        update = source * inv * (1.0 / theta)
        field = update
    else:
        remain = source - op_of(start)
        update = remain * inv * (1.0 / theta)
        field = start + update
    for index in range(steps - 1):
        rho_next = 1.0 / (2.0 * sigma - rho_now)
        remain = source - op_of(field)
        update = rho_next * rho_now * update + (2.0 * rho_next / delta) * (remain * inv)
        field = field + update
        rho_now = rho_next
    return field


def kernel(sizes, dims0, b_ref, c_ref, p_ref, q_ref, *scratch):
    (v0, ys0, zs0, xr0, yr0, zr0, ey0, v1, ys1, zs1, xr1, yr1, zr1, ey1, tile, slots,
     send0, recv0, send1, recv1, gsend, grecv) = scratch
    pos = tuple(lax.axis_index(a) for a in AXES)
    dims1 = tuple(d // 2 for d in dims0)
    dims2 = tuple(d // 2 for d in dims1)
    whole2 = tuple(d * n for d, n in zip(dims2, sizes))
    whole3 = tuple(d // 2 for d in whole2)
    nx, ny, nz = sizes
    count = nx * ny * nz
    me = (pos[0] * ny + pos[1]) * nz + pos[2]
    width2, width3 = upl(whole2[2]), upl(whole3[2])

    def coords(index):
        return (index // (ny * nz), (index // nz) % ny, index % nz)

    barrier = pltpu.get_barrier_semaphore()

    def greet(step, unused):
        pl.semaphore_signal(barrier, inc=1, device_id=coords((me + step) % count), device_id_type=MESH)
        return unused

    for ref in (xr0, yr0, zr0, xr1, yr1, zr1, ey0, ey1):
        ref[...] = jnp.zeros_like(ref)
    lax.fori_loop(1, count, greet, 0)

    def exists(axis, side):
        return pos[axis] > 0 if side == 0 else pos[axis] < sizes[axis] - 1

    def peer(axis, side):
        return tuple(p + ((-1, 1)[side] if a == axis else 0) for a, p in enumerate(pos))

    def copies(level, slot):
        x, y, z = (dims0, dims1)[level]
        rows = x * y
        v, ys, zs, xr, yr, zr, send, recv = (
            (v0, ys0, zs0, xr0, yr0, zr0, send0, recv0),
            (v1, ys1, zs1, xr1, yr1, zr1, send1, recv1),
        )[level]
        edge = up8(y)
        for axis in range(3):
            for side in range(2):
                if axis == 0:
                    start = 0 if side == 0 else rows - edge
                    src, dst = v.at[slot, pl.ds(start, edge)], xr.at[slot, 1 - side]
                elif axis == 1:
                    src, dst = ys.at[slot, side], yr.at[slot, 1 - side]
                else:
                    src, dst = zs.at[slot, side], zr.at[slot, 1 - side]
                yield axis, side, pltpu.make_async_remote_copy(
                    src_ref=src, dst_ref=dst,
                    send_sem=send.at[slot, 2 * axis + side],
                    recv_sem=recv.at[slot, 2 * axis + 1 - side],
                    device_id=peer(axis, side), device_id_type=MESH,
                )

    def launch(level, slot, wanted):
        for axis, side, copy in copies(level, slot):
            if axis in wanted:
                @pl.when(exists(axis, side))
                def _():
                    copy.start()

    def post(level, slot, value, now=True):
        x, y, z = (dims0, dims1)[level]
        rows = x * y
        v, ys, zs = ((v0, ys0, zs0), (v1, ys1, zs1))[level]
        v[slot] = value
        if now:
            launch(level, slot, (0,))
        for side in range(2):
            ys[slot, side] = v[slot, pl.ds(0 if side == 0 else y - 1, x, stride=y), :]
        if now:
            launch(level, slot, (1,))
        lane = iota((TILE, LANES), 1)
        for side in range(2):
            packed = jnp.zeros((TILE, LANES), F32)
            for t in range(rows // TILE):
                part = value[t * TILE:(t + 1) * TILE]
                shift = (t if side == 0 else t - (z - 1)) % LANES
                if shift:
                    part = pltpu.roll(part, shift, 1)
                packed = jnp.where(lane == t, part, packed)
            zs[slot, side] = packed
        if now:
            launch(level, slot, (2,))

    def drain(level, slot):
        for axis, side, copy in copies(level, slot):
            @pl.when(exists(axis, side))
            def _():
                copy.wait_send()

    def arrive(level, slot):
        xr, yr, zr, recv = ((xr0, yr0, zr0, recv0), (xr1, yr1, zr1, recv1))[level]
        for axis in range(3):
            for side in range(2):
                dst = (xr, yr, zr)[axis].at[slot, side]
                @pl.when(exists(axis, side))
                def _():
                    pltpu.make_async_copy(dst, dst, recv.at[slot, 2 * axis + side]).wait()

    def unpack(part, place, rows):
        out = []
        for t in range(rows // TILE):
            shift = (place - t) % LANES
            out.append(pltpu.roll(part, shift, 1) if shift else part)
        return jnp.concatenate(out, 0)

    def collect(level, slot, value):
        arrive(level, slot)
        x, y, z = (dims0, dims1)[level]
        rows = x * y
        xr, yr, zr, ey = ((xr0, yr0, zr0, ey0), (xr1, yr1, zr1, ey1))[level]
        edge = up8(y)
        below = jnp.concatenate([xr[slot, 0], value], 0)[edge - y:edge - y + rows]
        above = jnp.concatenate([value, xr[slot, 1]], 0)[y:y + rows]
        ey[slot, 0, pl.ds(0, x, stride=y), :] = yr[slot, 0]
        ey[slot, 1, pl.ds(y - 1, x, stride=y), :] = yr[slot, 1]
        row = mod(iota((rows, LANES), 0), y)
        lane = iota((rows, LANES), 1)
        left = jnp.where(row == 0, ey[slot, 0], pltpu.roll(value, 1, 0))
        right = jnp.where(row == y - 1, ey[slot, 1], pltpu.roll(value, rows - 1, 0))

        front = jnp.where(lane == 0, unpack(zr[slot, 0], 0, rows), pltpu.roll(value, 1, 1))
        back = jnp.where(lane == z - 1, unpack(zr[slot, 1], z - 1, rows), pltpu.roll(value, LANES - 1, 1))
        return (below, above, left, right, front, back)

    def local_edges(dims):
        x, y, z = dims
        rows = x * y
        plane, row, lane = div(iota((rows, LANES), 0), y), mod(iota((rows, LANES), 0), y), iota((rows, LANES), 1)
        return tuple(
            index + pos[axis] * dims[axis] == (0 if side == 0 else dims[axis] * sizes[axis] - 1)
            for axis, index in enumerate((plane, row, lane)) for side in range(2)
        )

    def whole_edges(dims, shape):
        x, y, z = dims
        plane, row, lane = div(iota(shape, 0), y), mod(iota(shape, 0), y), iota(shape, 1)
        return (plane == 0, plane == x - 1, row == 0, row == y - 1, lane == 0, lane >= z - 1)

    def whole_near(dims):
        x, y, z = dims
        rows = x * y

        def near(v):
            return (
                pltpu.roll(v, y, 0), pltpu.roll(v, rows - y, 0),
                pltpu.roll(v, 1, 0), pltpu.roll(v, rows - 1, 0),
                pltpu.roll(v, 1, 1), pltpu.roll(v, v.shape[1] - 1, 1),
            )
        return near

    def gather_copy(kind, step):
        target = coords((me + step) % count)
        return pltpu.make_async_remote_copy(
            src_ref=tile.at[kind], dst_ref=slots.at[kind, me],
            send_sem=gsend.at[kind], recv_sem=grecv.at[kind],
            device_id=target, device_id_type=MESH,
        )

    def gather_start(kind, value):
        tile[kind] = value

        def go(step, unused):
            gather_copy(kind, step).start()
            return unused
        lax.fori_loop(1, count, go, 0)

    def gather_finish(kind):
        part = slots.at[kind, pl.ds(0, count - 1)]
        pltpu.make_async_copy(part, part, grecv.at[kind]).wait()
        slots[kind, me] = tile[kind]
        per = LANES // dims2[2]
        block = dims2[0] * dims2[1]
        columns = []
        for lane_tile in range(width2 // LANES):
            rows = []
            for gx in range(nx):
                for gy in range(ny):
                    total = None
                    for gz in range(lane_tile * per, min((lane_tile + 1) * per, nz)):
                        part = slots[kind, (gx * ny + gy) * nz + gz]
                        total = part if total is None else total + part
                    rows.append(total)
            columns.append(jnp.concatenate(rows, 0))
        stacked = columns[0] if len(columns) == 1 else jnp.concatenate(columns, 1)
        n = whole2[0] * whole2[1]
        r, s = iota((n, n), 0), iota((n, n), 1)
        X, Y = div(r, whole2[1]), mod(r, whole2[1])
        want = (div(X, dims2[0]) * ny + div(Y, dims2[1])) * block + mod(X, dims2[0]) * dims2[1] + mod(Y, dims2[1])
        return pick_rows(chosen(s == want), stacked)

    offset = (pos[2] % (LANES // dims2[2])) * dims2[2]

    def fill(c, dims):
        return jnp.where(iota(c.shape, 1) < dims[2], c, 1.0)

    c0 = c_ref[...].reshape(dims0[0] * dims0[1], LANES)
    b0 = b_ref[...].reshape(dims0[0] * dims0[1], LANES)
    c1 = restrict(c0, dims0, LANES, 0)
    c2_own = restrict(c1, dims1, LANES, offset)
    c1 = fill(c1, dims1)
    post(0, 0, c0, False)
    post(1, 0, c1, False)
    pl.semaphore_wait(barrier, count - 1)

    launch(0, 0, (0, 1, 2))
    launch(1, 0, (0, 1, 2))
    gather_start(0, c2_own)

    lane0, row0, plane0 = (iota((dims0[0] * dims0[1], LANES), 1), mod(iota((dims0[0] * dims0[1], LANES), 0), dims0[1]),
                           div(iota((dims0[0] * dims0[1], LANES), 0), dims0[1]))
    sides0 = (plane0 == 0, plane0 == dims0[0] - 1, row0 == 0, row0 == dims0[1] - 1, lane0 == 0, lane0 == dims0[2] - 1)
    near0 = whole_near(dims0)
    near2, near3 = whole_near(whole2), whole_near(whole3)
    rows0, edge0 = dims0[0] * dims0[1], dims0[1]
    shape2 = (whole2[0] * whole2[1], width2)
    store = {}

    links0, total0, inv0 = make_coefs(c0, collect(0, 0, c0), local_edges(dims0), 1.0)
    inner0 = [jnp.where(side, 0.0, link) for side, link in zip(sides0, links0)]
    outer0 = [jnp.where(side, link, 0.0) for side, link in zip(sides0, links0)]

    def op0(slot, filler=None):
        def op(v):
            post(0, slot, v)
            out = apply_op(v, near0(v), (inner0, total0, None))
            if filler is not None:
                filler()
            arrive(0, slot)
            ey0[slot, 0, pl.ds(0, dims0[0], stride=edge0), :] = yr0[slot, 0]
            ey0[slot, 1, pl.ds(edge0 - 1, dims0[0], stride=edge0), :] = yr0[slot, 1]
            out = out - outer0[2] * ey0[slot, 0] - outer0[3] * ey0[slot, 1]
            out = out - outer0[4] * unpack(zr0[slot, 0], 0, rows0)
            out = out - outer0[5] * unpack(zr0[slot, 1], dims0[2] - 1, rows0)
            return jnp.concatenate([
                out[:edge0] - outer0[0][:edge0] * xr0[slot, 0],
                out[edge0:rows0 - edge0],
                out[rows0 - edge0:] - outer0[1][rows0 - edge0:] * xr0[slot, 1],
            ], 0)
        return op

    def ops(*steps):
        queue = list(steps)
        return lambda v: queue.pop(0)(v)

    def op1(slot, filler=None):
        def op(v):
            post(1, slot, v)
            if filler is not None:
                filler()
            store["near1"] = collect(1, slot, v)
            return apply_op(v, store["near1"], store["coefs1"])
        return op

    def fill_coefs1():
        store["coefs1"] = make_coefs(c1, collect(1, 0, c1), local_edges(dims1), 0.25)

    def fill_gather():
        store["c2"] = gather_finish(0)

    def fill_coefs2():
        c2 = store["c2"]
        store["c3"] = fill(restrict(c2, whole2, width3, 0), whole3)
        c2 = fill(c2, whole2)
        store["coefs2"] = make_coefs(c2, near2(c2), whole_edges(whole2, shape2), 0.25 ** 2)

    def fill_coefs3():
        c3 = store["c3"]
        store["coefs3"] = make_coefs(c3, near3(c3), whole_edges(whole3, c3.shape), 0.25 ** 3)
        store["prolong"] = prolong_near(
            dims1, shape2[0], width2, whole2[1], pos[0] * dims2[0], pos[1] * dims2[1], pos[2] * dims2[2])

    x0 = chebyshev(None, b0, 2, 0.3, 2.0, inv0, op0(1, fill_coefs1))
    r0 = b0 - op0(2, fill_gather)(x0)
    b1 = restrict(r0, dims0, LANES, 0)

    coefs1 = store["coefs1"]
    x1 = chebyshev(None, b1, 2, 0.3, 2.0, coefs1[2], op1(1, fill_coefs2))
    r1 = b1 - op1(2, fill_coefs3)(x1)
    gather_start(1, restrict(r1, dims1, LANES, offset))
    coefs2, coefs3, left5, rights = store["coefs2"], store["coefs3"], *store["prolong"]

    def op2(v):
        return apply_op(v, near2(v), coefs2)

    def op3(v):
        return apply_op(v, near3(v), coefs3)

    b2 = gather_finish(1)
    x2 = chebyshev(None, b2, 2, 0.3, 2.0, coefs2[2], op2)
    r2 = b2 - op2(x2)
    b3 = restrict(r2, whole2, width3, 0)
    x3 = chebyshev(None, b3, COARSE_DEGREE, 0.05, 2.0, coefs3[2], op3)
    x2 = x2 + prolong(x3, whole2, width2, whole3[1], 0, 0, 0)
    x2 = chebyshev(x2, b2, 2, 0.3, 2.0, coefs2[2], op2)

    rows1 = dims1[0] * dims1[1]
    picked = pick_rows(left5, x2)
    spread = pick_lanes(picked, rights[0])
    near_e = [spread[n * rows1:(n + 1) * rows1] for n in range(1, 5)] + [pick_lanes(picked[:rows1], m) for m in rights[1:]]
    near_x = store["near1"]

    def op1_known(v):
        return apply_op(v, [a + b for a, b in zip(near_x, near_e)], coefs1)

    x1 = x1 + spread[:rows1]
    x1 = chebyshev(x1, b1, 2, 0.3, 2.0, coefs1[2], ops(op1_known, op1(3)))
    x0 = x0 + prolong(x1, dims0, LANES, dims1[1], 0, 0, 0)
    x0 = chebyshev(x0, b0, 2, 0.3, 2.0, inv0, ops(op0(3), op0(4)))
    p_ref[...] = x0.reshape(p_ref.shape)
    res = b0 - op0(5)(x0)
    q_ref[...] = res.reshape(q_ref.shape)

    for slot in range(6):
        drain(0, slot)
    for slot in range(4):
        drain(1, slot)
    for kind in range(2):
        part = slots.at[kind, pl.ds(0, count - 1)]
        pltpu.make_async_copy(part, part, gsend.at[kind]).wait()


def solution(mesh):
    sizes = tuple(mesh.shape[a] for a in AXES)
    count = sizes[0] * sizes[1] * sizes[2]

    def per_device(b, c):
        dims0 = b.shape
        scratch = []
        for slots, (x, y, z) in ((6, dims0), (4, tuple(d // 2 for d in dims0))):
            scratch += [
                pltpu.VMEM((slots, x * y, LANES), F32),
                pltpu.VMEM((slots, 2, x, LANES), F32),
                pltpu.VMEM((slots, 2, TILE, LANES), F32),
                pltpu.VMEM((slots, 2, up8(y), LANES), F32),
                pltpu.VMEM((slots, 2, x, LANES), F32),
                pltpu.VMEM((slots, 2, TILE, LANES), F32),
                pltpu.VMEM((slots, 2, x * y, LANES), F32),
            ]
        scratch += [
            pltpu.VMEM((2, TILE, LANES), F32),
            pltpu.VMEM((2, count, TILE, LANES), F32),
            pltpu.SemaphoreType.DMA((6, 6)), pltpu.SemaphoreType.DMA((6, 6)),
            pltpu.SemaphoreType.DMA((4, 6)), pltpu.SemaphoreType.DMA((4, 6)),
            pltpu.SemaphoreType.DMA((2,)), pltpu.SemaphoreType.DMA((2,)),
        ]
        shape = jax.ShapeDtypeStruct(dims0, F32)
        return pl.pallas_call(
            functools.partial(kernel, sizes, dims0),
            out_shape=(shape, shape),
            in_specs=[pl.BlockSpec(memory_space=pltpu.VMEM)] * 2,
            out_specs=(pl.BlockSpec(memory_space=pltpu.VMEM),) * 2,
            scratch_shapes=scratch,
            compiler_params=pltpu.CompilerParams(collective_id=0, has_side_effects=True),
        )(b, c)

    spec = P(*AXES)
    return jax.shard_map(per_device, mesh=mesh, in_specs=(spec, spec), out_specs=(spec, spec), check_vma=False)
```
